32 devices in a mesh: freq: 4 (over y, x), clus: 8 (over z, core).
Axes of the slice: x: 2, y: 2, z: 4, core: 2. Of those that a mesh axis runs over, the one named last changes fastest.
Arguments:
- history: bfloat16 [1024, 8, 1024], P('freq', None, 'clus'), may hold values from -6 to 6
- near_blocks: bfloat16 [8, 4, 512, 2, 128, 128], P('clus', None, 'freq'), may hold values from -0.1875 to 0.1875
- near_list: int32 [8, 4], replicated, may hold values from 0 to 7, as said below
- basis_out: bfloat16 [512, 2, 32, 1024], P('freq', None, None, 'clus'), may hold values from -0.75 to 0.75
- basis_in: bfloat16 [512, 2, 32, 1024], P('freq', None, None, 'clus'), may hold values from -0.375 to 0.375
- coupling: bfloat16 [8, 512, 2, 32, 256], P('clus', 'freq'), may hold values from -0.375 to 0.375
- ranks: int32 [8, 512, 8], P('clus', 'freq'), may hold values from 4 to 32
Outputs:
- potential: bfloat16 [512, 2, 8, 1024], P('freq', None, None, 'clus')
The draws below stay inside these ranges and needn't reach their ends.
Inputs may be any that keep to these rules, and one draw needn't show every extreme that they name: `near_list`: row t starts with t itself; its other 3 entries are distinct shards other than t, each (t + d) mod 8 for some d with 1 <= |d| <= 3.
All inputs are finite; a program needn't handle non-finite values.
Results may differ from the reference program's by a relative error of at most 0.0055.
Values may be sent and summed in bfloat16 or wider, within the bound.
A program may use at most 128 MiB of HBM per device.

```python
import math
import jax
import jax.numpy as jnp
from jax import lax

STEPS = 1024
WAVES = 512
EXC = 8
PC = 128
NEAR = 4
RANK = 32
NPAN = 1024
N_CLUS = 8


def draw_near_list(key, part):
    reach = NEAR - 1

    def one_row(target):
        order = jax.random.permutation(jax.random.fold_in(key, target), 2 * reach)[:reach].astype(jnp.int32)
        offsets = jnp.where(order < reach, order + 1, reach - 1 - order)
        others = (target + offsets + N_CLUS) % N_CLUS
        return jnp.concatenate([jnp.reshape(target, (1,)).astype(jnp.int32), others.astype(jnp.int32)])
    return jax.vmap(one_row)(lax.iota(jnp.int32, N_CLUS))


def place_ends(drawn, own_key, smallest, top_value):
    longest = drawn.shape.index(max(drawn.shape))
    spots = []
    for shift in (0, 1):
        where = [jax.random.randint(jax.random.fold_in(own_key, axis), (), 0, length) for axis, length in enumerate(drawn.shape)]
        where[longest] = (where[longest] + shift) % drawn.shape[longest]
        spots.append(tuple(where))
    return drawn.at[spots[0]].set(smallest).at[spots[1]].set(top_value)


def shard_levels(stream_key, dims, pieces, least, largest):
    gain = 1.0
    for axis_at, blocks in pieces:
        draws = jax.random.uniform(jax.random.fold_in(jax.random.fold_in(stream_key, 6), axis_at), (blocks,), jnp.float32, least / len(pieces), largest / len(pieces))
        gain = gain * jnp.repeat(jnp.exp(draws), dims[axis_at] // blocks).reshape((-1,) + (1,) * (len(dims) - 1 - axis_at))
    return gain


def centred(rng, extent, deviation, most, cuts=(), held_as=jnp.bfloat16):
    entries = deviation * jax.random.normal(rng, extent, jnp.float32)
    if cuts:
        entries = entries * shard_levels(rng, extent, cuts, -0.22, 0.18)
    return jnp.clip(entries, -most, most).astype(held_as)


def setup_inputs(seed: int = 0) -> dict:
    arg_keys = jax.random.split(jax.random.key(seed), 8)
    return {
        "history": centred(arg_keys[0], (STEPS, EXC, NPAN), 1.0, 6.0, ((0, 4), (2, 8))),
        "near_blocks": centred(arg_keys[1], (N_CLUS, NEAR, WAVES, 2, PC, PC), (2 * NEAR * PC) ** -0.5, 0.1875, ((0, 8), (2, 4))),
        "near_list": draw_near_list(jax.random.fold_in(arg_keys[7], 71), 0),
        "basis_out": centred(arg_keys[3], (WAVES, 2, RANK, NPAN), (2 * RANK) ** -0.5, 0.75, ((0, 4), (3, 8))),
        "basis_in": centred(arg_keys[4], (WAVES, 2, RANK, NPAN), (2 * PC) ** -0.5, 0.375, ((0, 4), (3, 8))),
        "coupling": centred(arg_keys[5], (N_CLUS, WAVES, 2, RANK, N_CLUS * RANK), (RANK * N_CLUS) ** -0.5, 0.375, ((0, 8), (1, 4))),
        "ranks": place_ends(jax.random.randint(arg_keys[6], (N_CLUS, WAVES, N_CLUS), RANK // 8, RANK + 1), jax.random.fold_in(arg_keys[6], 1), RANK // 8, RANK).astype(jnp.int32),
    }


def wave_table(first_wave, count, first_step, length, total):
    waves = first_wave + lax.iota(jnp.int32, count)
    steps = first_step + lax.iota(jnp.int32, length)
    phase = (waves[:, None] * steps[None, :]) % total
    angle = phase.astype(jnp.float32) * (2.0 * math.pi / total)
    weight = jnp.exp(steps.astype(jnp.float32) * (-math.log(2.0) / total)) * (total ** -0.5)
    return weight[None, :] * jnp.cos(angle), -weight[None, :] * jnp.sin(angle)


def transform(history, cos_tab, sin_tab):
    flat = history.reshape(history.shape[0], -1).astype(jnp.float32)
    real_part = jnp.dot(cos_tab, flat, precision=lax.Precision.HIGHEST)
    imag_part = jnp.dot(sin_tab, flat, precision=lax.Precision.HIGHEST)
    return jnp.stack([real_part, imag_part], 1).reshape(cos_tab.shape[0], 2, history.shape[1], history.shape[2])


def complex_product(form, left_re, left_im, right_re, right_im):
    def product(left, right):
        return jnp.einsum(form, left.astype(jnp.float32), right.astype(jnp.float32))
    return product(left_re, right_re) - product(left_im, right_im), product(left_re, right_im) + product(left_im, right_re)


def far_mask(limit, nearby, clusters, rank):
    position = lax.iota(jnp.int32, rank)
    keep_out = position[None, None, :] < limit[:, :, None]
    keep_in = keep_out & jnp.logical_not(nearby)[None, :, None]
    mask = jnp.transpose(keep_out, (0, 2, 1))[:, :, :, None] & keep_in[:, None, :, :]
    return mask.reshape(limit.shape[0], rank, clusters * rank)


def reference(history, near_blocks, near_list, basis_out, basis_in, coupling, ranks):
    cos_tab, sin_tab = wave_table(0, WAVES, 0, STEPS, STEPS)
    dens = transform(history, cos_tab, sin_tab).astype(jnp.bfloat16)
    spaced = dens.reshape(WAVES, 2, EXC, N_CLUS, PC)
    basis = basis_in.reshape(WAVES, 2, RANK, N_CLUS, PC)
    coeff_re, coeff_im = complex_product("krsp,kesp->kesr", basis[:, 0], basis[:, 1], spaced[:, 0], spaced[:, 1])
    coeffs = jnp.stack([coeff_re, coeff_im], 1).astype(jnp.bfloat16)
    stacked = coeffs.reshape(WAVES, 2, EXC, N_CLUS * RANK)
    cluster_ids = lax.iota(jnp.int32, N_CLUS)
    outputs = []
    for target in range(N_CLUS):
        chosen = jnp.stack([lax.dynamic_slice_in_dim(dens, (near_list[target, slot] * PC).astype(jnp.int32), PC, 3) for slot in range(NEAR)])
        blocks = near_blocks[target]
        near_re, near_im = complex_product("jkpq,jkeq->kep", blocks[:, :, 0], blocks[:, :, 1], chosen[:, :, 0], chosen[:, :, 1])
        nearby = jnp.any(near_list[target][:, None] == cluster_ids[None, :], axis=0)
        mask = far_mask(ranks[target], nearby, N_CLUS, RANK)
        couple = coupling[target]
        couple_re = jnp.where(mask, couple[:, 0], jnp.zeros_like(couple[:, 0]))
        couple_im = jnp.where(mask, couple[:, 1], jnp.zeros_like(couple[:, 1]))
        mixed_re, mixed_im = complex_product("kim,kem->kei", couple_re, couple_im, stacked[:, 0], stacked[:, 1])
        mixed_re = mixed_re.astype(jnp.bfloat16)
        mixed_im = mixed_im.astype(jnp.bfloat16)
        out_basis = basis_out[:, :, :, target * PC:(target + 1) * PC]
        far_re, far_im = complex_product("kip,kei->kep", out_basis[:, 0], out_basis[:, 1], mixed_re, mixed_im)
        outputs.append(jnp.stack([near_re + far_re, near_im + far_im], 1).astype(jnp.bfloat16))
    return jnp.concatenate(outputs, axis=3)
```

```python
import functools
import math

import jax
import jax.numpy as jnp
from jax import lax
from jax.experimental import pallas as pl
from jax.experimental.pallas import tpu as pltpu
from jax.sharding import PartitionSpec as P

LANES = 128
NT = (((1,), (1,)), ((), ()))
NN = (((1,), (0,)), ((), ()))


def dot(left, right, dims):
    return lax.dot_general(left, right, dims, preferred_element_type=jnp.float32)


def wave_factors(first_wave, count, total):
    waves = (first_wave + lax.iota(jnp.int32, count))[:, None]

    def factor(steps, scale):
        angle = (waves * steps[None, :] % total).astype(jnp.float32) * (2.0 * math.pi / total)
        weight = jnp.exp(steps.astype(jnp.float32) * (-math.log(2.0) / total)) * scale
        return weight[None, :] * jnp.cos(angle), -weight[None, :] * jnp.sin(angle)

    coarse = factor(lax.iota(jnp.int32, total // LANES) * LANES, 1.0)
    fine = factor(lax.iota(jnp.int32, LANES), total ** (-0.5))
    return coarse + fine


def fill_tables(coarse_re, coarse_im, fine_re, fine_im, high, low):
    count = fine_re.shape[0]
    for a in range(coarse_re.shape[1]):
        c_re, c_im = coarse_re[:, a : a + 1], coarse_im[:, a : a + 1]
        f_re, f_im = fine_re[...], fine_im[...]
        for part, value in ((0, c_re * f_re - c_im * f_im), (1, c_re * f_im + c_im * f_re)):
            top = value.astype(jnp.bfloat16)
            rows, cols = pl.ds(part * count, count), pl.ds(a * LANES, LANES)
            high[rows, cols] = top
            low[rows, cols] = (value - top.astype(jnp.float32)).astype(jnp.bfloat16)


def transform_one(e, hist, high, low, sums):
    blocks, length = hist.shape[0], hist.shape[2]
    waves = high.shape[0] // 2
    exc = hist.shape[1]
    steps = jnp.concatenate([hist[f, e] for f in range(blocks)], axis=0)
    value = dot(high[...], steps, NN) + dot(low[...], steps, NN)
    for part in range(2):
        sums[pl.ds(part * exc + e, waves, stride=2 * exc), :] = value[part * waves : (part + 1) * waves]


def compress(group, pack, dens, basis_in, coeffs):
    rows, rank = dens.shape[1], basis_in.shape[2]
    half = rows // 2
    waves = pl.ds(group * pack, pack)
    left = dens[waves].reshape(pack * rows, LANES)
    lane = lax.broadcasted_iota(jnp.int32, (rows, LANES), 1) // rank

    def pick(part):
        full = dot(left, basis_in[waves, part].reshape(pack * rank, LANES), NT)
        out = full[:rows]
        for w in range(1, pack):
            out = jnp.where(lane == w, full[w * rows : (w + 1) * rows], out)
        return out

    by_re, by_im = pick(0), pick(1)
    real = by_re[:half] - by_im[half:]
    imag = by_re[half:] + by_im[:half]
    coeffs[group] = jnp.concatenate([real, imag], 0).astype(jnp.bfloat16)


def transform_kernel(c_re, c_im, f_re, f_im, hist, basis_in, dens, coeffs, high, low, sums):
    fill_tables(c_re, c_im, f_re, f_im, high, low)
    for e in range(hist.shape[1]):
        transform_one(e, hist, high, low, sums)
    dens[...] = sums[...].reshape(dens.shape).astype(jnp.bfloat16)
    pack = LANES // basis_in.shape[2]

    def step(group, carry):
        compress(group, pack, dens, basis_in, coeffs)
        return carry

    lax.fori_loop(0, coeffs.shape[0], step, 0)


def apply_kernel(mine, near, dens, coeffs, couple, basis_out, limit, out):
    slots, waves = near.shape[1], near.shape[2]
    panels, rank = near.shape[4], couple.shape[3]
    sources, rows = dens.shape[0], dens.shape[2]
    half = rows // 2
    pack = LANES // rank
    picked = [mine[j] for j in range(slots)]
    position = lax.broadcasted_iota(jnp.int32, (rank, sources * rank), 0)

    def step(group, carry):
        packed = [coeffs[s, group].astype(jnp.float32) for s in range(sources)]
        for w in range(pack):
            k = group * pack + w
            left = jnp.concatenate([dens[s, k] for s in picked], axis=1)
            right = jnp.concatenate(
                [near[0, j, k].reshape(2 * panels, panels) for j in range(slots)], axis=1
            )
            both = dot(left, right, NT)
            stacked = jnp.concatenate(
                [p[:, w * rank : (w + 1) * rank] for p in packed], axis=1
            ).astype(jnp.bfloat16)
            keep = position < limit[pl.ds(k, 1), :]

            def mix(part):
                value = couple[0, k, part]
                return dot(stacked, jnp.where(keep, value, jnp.zeros_like(value)), NT)

            by_re, by_im = mix(0), mix(1)
            mixed = jnp.concatenate(
                [by_re[:half] - by_im[half:], by_re[half:] + by_im[:half]], 0
            ).astype(jnp.bfloat16)
            spread = jnp.concatenate([basis_out[k, 0], basis_out[k, 1]], axis=1)
            both = both + dot(mixed, spread, NN)
            by_re, by_im = both[:, :panels], both[:, panels:]
            out[k, 0] = (by_re[:half] - by_im[half:]).astype(out.dtype)
            out[k, 1] = (by_re[half:] + by_im[:half]).astype(out.dtype)
        return carry

    lax.fori_loop(0, waves // pack, step, 0)


def apply_all(mine, near_blocks, dens, coeffs, coupling, basis_out, limit):
    waves, panels = basis_out.shape[0], basis_out.shape[3]
    rank, slots = basis_out.shape[2], near_blocks.shape[1]
    sources, _, rows, _ = dens.shape
    step = min(waves, 8)
    pack = LANES // rank
    grid_spec = pltpu.PrefetchScalarGridSpec(
        num_scalar_prefetch=1,
        grid=(waves // step,),
        in_specs=[
            pl.BlockSpec((1, slots, step, 2, panels, panels), lambda g, m: (0, 0, g, 0, 0, 0)),
            pl.BlockSpec((sources, step, rows, panels), lambda g, m: (0, g, 0, 0)),
            pl.BlockSpec((sources, step // pack, rows, LANES), lambda g, m: (0, g, 0, 0)),
            pl.BlockSpec((1, step, 2, rank, sources * rank), lambda g, m: (0, g, 0, 0, 0)),
            pl.BlockSpec((step, 2, rank, panels), lambda g, m: (g, 0, 0, 0)),
            pl.BlockSpec((step, sources * rank), lambda g, m: (g, 0)),
        ],
        out_specs=pl.BlockSpec((step, 2, rows // 2, panels), lambda g, m: (g, 0, 0, 0)),
    )
    return pl.pallas_call(
        apply_kernel,
        out_shape=jax.ShapeDtypeStruct((waves, 2, rows // 2, panels), jnp.bfloat16),
        grid_spec=grid_spec,
    )(mine, near_blocks, dens, coeffs, coupling, basis_out, limit)


def local(history, near_blocks, near_list, basis_out, basis_in, coupling, ranks):
    steps_dev, exc, panels = history.shape
    waves_dev, _, rank, _ = basis_in.shape
    clusters = lax.axis_size("clus")
    freqs = lax.axis_size("freq")
    total = steps_dev * freqs
    pack = LANES // rank
    mine = lax.dynamic_index_in_dim(near_list, lax.axis_index("clus"), 0, keepdims=False)
    nearby = jnp.any(mine[:, None] == lax.iota(jnp.int32, clusters)[None, :], axis=0)
    far = jnp.where(nearby[None, :], 0, ranks[0])
    within = lax.iota(jnp.int32, rank)
    limit = jnp.where(within[None, None, :] < far[:, :, None], far[:, :, None], 0)
    limit = limit.reshape(waves_dev, clusters * rank)
    factors = wave_factors(lax.axis_index("freq") * waves_dev, waves_dev, total)
    turned = jnp.transpose(history, (1, 0, 2))
    hist = lax.all_gather(turned, "freq", axis=0)
    dens, coeffs = pl.pallas_call(
        transform_kernel,
        out_shape=(
            jax.ShapeDtypeStruct((waves_dev, 2 * exc, panels), jnp.bfloat16),
            jax.ShapeDtypeStruct((waves_dev // pack, 2 * exc, LANES), jnp.bfloat16),
        ),
        scratch_shapes=[
            pltpu.VMEM((2 * waves_dev, total), jnp.bfloat16),
            pltpu.VMEM((2 * waves_dev, total), jnp.bfloat16),
            pltpu.VMEM((waves_dev * 2 * exc, panels), jnp.float32),
        ],
    )(*factors, hist, basis_in)
    dens = lax.all_gather(dens, "clus", axis=0)
    coeffs = lax.all_gather(coeffs, "clus", axis=0)
    return apply_all(mine, near_blocks, dens, coeffs, coupling, basis_out, limit)


def solution(mesh):
    placed = (
        P("freq", None, "clus"),
        P("clus", None, "freq", None, None, None),
        P(),
        P("freq", None, None, "clus"),
        P("freq", None, None, "clus"),
        P("clus", "freq", None, None, None),
        P("clus", "freq", None),
    )
    return jax.shard_map(
        local, mesh=mesh, in_specs=placed, out_specs=P("freq", None, None, "clus"), check_vma=False
    )
```

```python
import functools
import math

import jax
import jax.numpy as jnp
from jax import lax
from jax.experimental import pallas as pl
from jax.experimental.pallas import tpu as pltpu
from jax.sharding import PartitionSpec as P

LANES = 128
NT = (((1,), (1,)), ((), ()))
NN = (((1,), (0,)), ((), ()))


def dot(left, right, dims):
    return lax.dot_general(left, right, dims, preferred_element_type=jnp.float32)


def wave_factors(first_wave, count, total):
    waves = (first_wave + lax.iota(jnp.int32, count))[:, None]

    def factor(steps, scale):
        angle = (waves * steps[None, :] % total).astype(jnp.float32) * (2.0 * math.pi / total)
        weight = jnp.exp(steps.astype(jnp.float32) * (-math.log(2.0) / total)) * scale
        return weight[None, :] * jnp.cos(angle), -weight[None, :] * jnp.sin(angle)

    coarse = factor(lax.iota(jnp.int32, total // LANES) * LANES, 1.0)
    fine = factor(lax.iota(jnp.int32, LANES), total ** (-0.5))
    return coarse + fine


CHUNKS = 4
MESH = pl.DeviceIdType.MESH


def fill_tables(coarse_re, coarse_im, fine_re, fine_im, table):
    waves = fine_re.shape[0]
    chunk = waves // CHUNKS
    for a in range(coarse_re.shape[1]):
        c_re, c_im = coarse_re[:, a : a + 1], coarse_im[:, a : a + 1]
        f_re, f_im = fine_re[...], fine_im[...]
        for part, value in ((0, c_re * f_re - c_im * f_im), (1, c_re * f_im + c_im * f_re)):
            high = value.astype(jnp.bfloat16)
            low = (value - high.astype(jnp.float32)).astype(jnp.bfloat16)
            for w in range(CHUNKS):
                for piece, held in ((0, high), (1, low)):
                    rows = pl.ds((2 * piece + part) * chunk, chunk)
                    table[w, rows, a * LANES : (a + 1) * LANES] = held[w * chunk : (w + 1) * chunk]


def transform_chunk(w, hist, table, sums, buf, me):
    blocks, exc, length = hist.shape[0], hist.shape[1], hist.shape[2]
    half = table.shape[1] // 2
    chunk = half // 2
    for e in range(0, exc, 2):
        value = None
        for f in range(blocks):
            steps = jnp.concatenate([hist[f, e], hist[f, e + 1]], axis=1)
            term = dot(table[w, :, f * length : (f + 1) * length], steps, NN)
            value = term if value is None else value + term
        value = value[:half] + value[half:]
        for part in range(2):
            for side in range(2):
                sums[pl.ds(part * exc + e + side, chunk, stride=2 * exc), :] = value[
                    part * chunk : (part + 1) * chunk, side * LANES : (side + 1) * LANES
                ]
    buf[me, pl.ds(0, chunk)] = sums[...].reshape(chunk, 2 * exc, LANES).astype(jnp.bfloat16)


def compress_chunk(w, buf, basis_in, me, chunk):
    rows, rank = buf.shape[2], basis_in.shape[2]
    half = rows // 2
    pack = LANES // rank
    lane = lax.broadcasted_iota(jnp.int32, (rows, LANES), 1) // rank

    def step(group, carry):
        left = buf[me, pl.ds(group * pack, pack)].reshape(pack * rows, LANES)

        def pick(part):
            right = basis_in[pl.ds(w * chunk + group * pack, pack), part]
            full = dot(left, right.reshape(pack * rank, LANES), NT)
            out = full[:rows]
            for i in range(1, pack):
                out = jnp.where(lane == i, full[i * rows : (i + 1) * rows], out)
            return out

        by_re, by_im = pick(0), pick(1)
        real = by_re[:half] - by_im[half:]
        imag = by_re[half:] + by_im[:half]
        buf[me, chunk + group] = jnp.concatenate([real, imag], 0).astype(jnp.bfloat16)
        return carry

    lax.fori_loop(0, chunk // pack, step, 0)


def apply_chunk(w, picked, near, buf, couple, basis_out, limit, out):
    slots, chunk = near.shape[1], near.shape[2]
    panels, rank = near.shape[4], couple.shape[2]
    sources, rows = buf.shape[0], buf.shape[2]
    half = rows // 2
    pack = LANES // rank
    position = lax.broadcasted_iota(jnp.int32, (rank, sources * rank), 0)

    def step(group, carry):
        packed = [buf[s, chunk + group].astype(jnp.float32) for s in range(sources)]
        for i in range(pack):
            k = group * pack + i
            wave = w * chunk + k
            left = jnp.concatenate([buf[s, k] for s in picked], axis=1)
            right = jnp.concatenate(
                [near[w, j, k].reshape(2 * panels, panels) for j in range(slots)], axis=1
            )
            both = dot(left, right, NT)
            stacked = jnp.concatenate(
                [p[:, i * rank : (i + 1) * rank] for p in packed], axis=1
            ).astype(jnp.bfloat16)
            keep = position < limit[pl.ds(wave, 1), :]

            def mix(part):
                value = couple[wave, part]
                return dot(stacked, jnp.where(keep, value, jnp.zeros_like(value)), NT)

            by_re, by_im = mix(0), mix(1)
            mixed = jnp.concatenate(
                [by_re[:half] - by_im[half:], by_re[half:] + by_im[:half]], 0
            ).astype(jnp.bfloat16)
            spread = jnp.concatenate([basis_out[wave, 0], basis_out[wave, 1]], axis=1)
            both = both + dot(mixed, spread, NN)
            by_re, by_im = both[:, :panels], both[:, panels:]
            out[wave, 0] = (by_re[:half] - by_im[half:]).astype(out.dtype)
            out[wave, 1] = (by_re[half:] + by_im[:half]).astype(out.dtype)
        return carry

    lax.fori_loop(0, chunk // pack, step, 0)


def kernel(freqs, clusters, mine, c_re, c_im, f_re, f_im, limit, own, near_in, couple_in, out_in, in_in,
           out, hist, table, sums, near, couple, basis_out, basis_in, *rest):
    bufs = rest[:CHUNKS]
    local_sem, near_sem, hist_send, hist_recv, send_sem, recv_sem = rest[CHUNKS:]
    f, c = lax.axis_index("freq"), lax.axis_index("clus")
    z, core = c // 2, c % 2
    levels = clusters // 2
    has_up, has_down = z + 1 < levels, z > 0
    up, down, partner = c + 2, c - 2, c + 1 - 2 * core
    chunk = near.shape[2]
    square = freqs == 4
    beside, across = f + 1 - 2 * (f % 2), (f + 2) % freqs
    peers = [beside, across] if square else [(f + i) % freqs for i in range(1, freqs)]

    loads = [
        pltpu.make_async_copy(own, hist.at[f], local_sem.at[0]),
        pltpu.make_async_copy(in_in, basis_in, local_sem.at[1]),
        pltpu.make_async_copy(out_in, basis_out, local_sem.at[2]),
        pltpu.make_async_copy(couple_in.at[0], couple, local_sem.at[3]),
    ]
    blocks = [
        pltpu.make_async_copy(near_in.at[0, :, pl.ds(w * chunk, chunk)], near.at[w], near_sem.at[w])
        for w in range(CHUNKS)
    ]

    barrier = pltpu.get_barrier_semaphore()
    for peer in peers:
        pl.semaphore_signal(barrier, inc=1, device_id=(peer, c), device_id_type=MESH)
    pl.semaphore_signal(barrier, inc=1, device_id=(f, partner), device_id_type=MESH)

    @pl.when(has_up)
    def _():
        pl.semaphore_signal(barrier, inc=1, device_id=(f, up), device_id_type=MESH)

    @pl.when(has_down)
    def _():
        pl.semaphore_signal(barrier, inc=1, device_id=(f, down), device_id_type=MESH)

    loads[0].start()
    pl.semaphore_wait(barrier, len(peers) + 1 + jnp.where(z + 1 < levels, 1, 0) + jnp.where(z > 0, 1, 0))

    exc = own.shape[0]
    halves = [pl.ds(0, exc // 2), pl.ds(exc // 2, exc // 2)]

    def give(peer, slot, part, source, number):
        return pltpu.make_async_remote_copy(
            src_ref=source, dst_ref=hist.at[slot, halves[part]],
            send_sem=hist_send.at[number], recv_sem=hist_recv.at[slot, part],
            device_id=(peer, c), device_id_type=MESH,
        )

    def arrived(slot, part):
        give(peers[0], slot, part, hist.at[slot, halves[part]], 0).wait_recv()

    sent = []
    for number, peer in enumerate(peers):
        for part in ((0, 1) if number % 2 == 0 else (1, 0)):
            sent.append(give(peer, f, part, own.at[halves[part]], 2 * number + part))
            sent[-1].start()
    for copy in loads[1:] + blocks:
        copy.start()
    fill_tables(c_re, c_im, f_re, f_im, table)
    if square:
        arrived(beside, 0)
        sent.append(give(across, beside, 0, hist.at[beside, halves[0]], 4))
        sent[-1].start()
        arrived(across, 1)
        sent.append(give(beside, across, 1, hist.at[across, halves[1]], 5))
        sent[-1].start()
        corner = (beside + 2) % freqs
        for slot, part in ((beside, 1), (across, 0), (corner, 0), (corner, 1)):
            arrived(slot, part)
    else:
        for peer in peers:
            for part in range(2):
                arrived(peer, part)
    for copy in sent:
        copy.wait_send()
    loads[0].wait()
    loads[1].wait()

    def pass_on(w, source, target, way):
        return pltpu.make_async_remote_copy(
            src_ref=bufs[w].at[source], dst_ref=bufs[w].at[source],
            send_sem=send_sem.at[w, source // 2, way], recv_sem=recv_sem.at[w, source],
            device_id=(f, target), device_id_type=MESH,
        )

    def when(flag, action):
        @pl.when(flag)
        def _():
            action()

    for w in range(CHUNKS):
        transform_chunk(w, hist, table, sums, bufs[w], c)
        compress_chunk(w, bufs[w], basis_in, c, chunk)
        when(has_up, lambda: pass_on(w, c, up, 0).start())
        when(has_down, lambda: pass_on(w, c, down, 1).start())
        pass_on(w, c, partner, 2).start()

    for copy in loads[2:]:
        copy.wait()
    picked = [mine[j] for j in range(near.shape[1])]
    for d in range(1, levels):
        for w in range(CHUNKS):
            below, above = c - 2 * d, c + 2 * d

            def from_below():
                pass_on(w, below, partner, 2).wait_recv()
                when(has_up, lambda: pass_on(w, below, up, 0).start())
                pass_on(w, below, partner, 2).start()

            def from_above():
                pass_on(w, above, partner, 2).wait_recv()
                when(has_down, lambda: pass_on(w, above, down, 1).start())
                pass_on(w, above, partner, 2).start()

            when(z >= d, from_below)
            when(z + d < levels, from_above)
    for w in range(CHUNKS):
        pass_on(w, partner, partner, 2).wait_recv()
        for d in range(1, levels):
            below, above = partner - 2 * d, partner + 2 * d
            when(z >= d, lambda: pass_on(w, below, partner, 2).wait_recv())
            when(z + d < levels, lambda: pass_on(w, above, partner, 2).wait_recv())
        blocks[w].wait()
        apply_chunk(w, picked, near, bufs[w], couple, basis_out, limit, out)

    for w in range(CHUNKS):
        when(has_up, lambda: pass_on(w, c, up, 0).wait_send())
        when(has_down, lambda: pass_on(w, c, down, 1).wait_send())
        pass_on(w, c, partner, 2).wait_send()
        for d in range(1, levels):
            below, above = c - 2 * d, c + 2 * d

            def below_sent():
                when(has_up, lambda: pass_on(w, below, up, 0).wait_send())
                pass_on(w, below, partner, 2).wait_send()

            def above_sent():
                when(has_down, lambda: pass_on(w, above, down, 1).wait_send())
                pass_on(w, above, partner, 2).wait_send()

            when(z >= d, below_sent)
            when(z + d < levels, above_sent)


def step_all(mine, factors, limit, turned, near_blocks, coupling, basis_out, basis_in, freqs, clusters):
    exc, length, panels = turned.shape
    waves, _, rank, _ = basis_in.shape
    slots = near_blocks.shape[1]
    chunk = waves // CHUNKS
    pack = LANES // rank
    rows = 2 * exc
    bf16 = jnp.bfloat16
    vmem, anywhere = pl.BlockSpec(memory_space=pltpu.VMEM), pl.BlockSpec(memory_space=pl.ANY)
    dma = pltpu.SemaphoreType.DMA
    return pl.pallas_call(
        functools.partial(kernel, freqs, clusters),
        out_shape=jax.ShapeDtypeStruct((waves, 2, exc, panels), bf16),
        in_specs=[pl.BlockSpec(memory_space=pltpu.SMEM)] + [vmem] * 6 + [anywhere] * 4,
        out_specs=vmem,
        scratch_shapes=[
            pltpu.VMEM((freqs, exc, length, panels), bf16),
            pltpu.VMEM((CHUNKS, 4 * chunk, freqs * length), bf16),
            pltpu.VMEM((chunk * rows, panels), jnp.float32),
            pltpu.VMEM((CHUNKS, slots, chunk, 2, panels, panels), bf16),
            pltpu.VMEM(coupling.shape[1:], bf16),
            pltpu.VMEM(basis_out.shape, bf16),
            pltpu.VMEM(basis_in.shape, bf16),
        ]
        + [pltpu.VMEM((clusters, chunk + chunk // pack, rows, panels), bf16)] * CHUNKS
        + [
            dma((4,)),
            dma((CHUNKS,)),
            dma((max(6, 2 * freqs),)),
            dma((freqs, 2)),
            dma((CHUNKS, clusters // 2, 3)),
            dma((CHUNKS, clusters)),
        ],
        compiler_params=pltpu.CompilerParams(
            collective_id=0, has_side_effects=True, vmem_limit_bytes=60 * 1024 * 1024
        ),
    )(mine, *factors, limit, turned, near_blocks, coupling, basis_out, basis_in)


def local(history, near_blocks, near_list, basis_out, basis_in, coupling, ranks):
    steps_dev, exc, panels = history.shape
    waves_dev, _, rank, _ = basis_in.shape
    clusters = lax.axis_size("clus")
    freqs = lax.axis_size("freq")
    total = steps_dev * freqs
    mine = lax.dynamic_index_in_dim(near_list, lax.axis_index("clus"), 0, keepdims=False)
    nearby = jnp.any(mine[:, None] == lax.iota(jnp.int32, clusters)[None, :], axis=0)
    far = jnp.where(nearby[None, :], 0, ranks[0])
    within = lax.iota(jnp.int32, rank)
    limit = jnp.where(within[None, None, :] < far[:, :, None], far[:, :, None], 0)
    limit = limit.reshape(waves_dev, clusters * rank)
    factors = wave_factors(lax.axis_index("freq") * waves_dev, waves_dev, total)
    turned = jnp.transpose(history, (1, 0, 2))
    return step_all(
        mine, factors, limit, turned, near_blocks, coupling, basis_out, basis_in, freqs, clusters
    )


def solution(mesh):
    placed = (
        P("freq", None, "clus"),
        P("clus", None, "freq", None, None, None),
        P(),
        P("freq", None, None, "clus"),
        P("freq", None, None, "clus"),
        P("clus", "freq", None, None, None),
        P("clus", "freq", None),
    )
    return jax.shard_map(
        local, mesh=mesh, in_specs=placed, out_specs=P("freq", None, None, "clus"), check_vma=False
    )
```

```python
import functools
import math

import jax
import jax.numpy as jnp
from jax import lax
from jax.experimental import pallas as pl
from jax.experimental.pallas import tpu as pltpu
from jax.sharding import PartitionSpec as P

LANES = 128
NT = (((1,), (1,)), ((), ()))
NN = (((1,), (0,)), ((), ()))


def dot(left, right, dims):
    return lax.dot_general(left, right, dims, preferred_element_type=jnp.float32)


def wave_factors(first_wave, count, total):
    waves = (first_wave + lax.iota(jnp.int32, count))[:, None]

    def factor(steps, scale):
        angle = (waves * steps[None, :] % total).astype(jnp.float32) * (2.0 * math.pi / total)
        weight = jnp.exp(steps.astype(jnp.float32) * (-math.log(2.0) / total)) * scale
        return weight[None, :] * jnp.cos(angle), -weight[None, :] * jnp.sin(angle)

    coarse = factor(lax.iota(jnp.int32, total // LANES) * LANES, 1.0)
    fine = factor(lax.iota(jnp.int32, LANES), total ** (-0.5))
    return coarse + fine


CHUNKS = 4
MESH = pl.DeviceIdType.MESH


def fill_tables(coarse_re, coarse_im, fine_re, fine_im, table):
    waves = fine_re.shape[0]
    chunk = waves // CHUNKS
    for a in range(coarse_re.shape[1]):
        c_re, c_im = coarse_re[:, a : a + 1], coarse_im[:, a : a + 1]
        f_re, f_im = fine_re[...], fine_im[...]
        for part, value in ((0, c_re * f_re - c_im * f_im), (1, c_re * f_im + c_im * f_re)):
            high = value.astype(jnp.bfloat16)
            low = (value - high.astype(jnp.float32)).astype(jnp.bfloat16)
            for w in range(CHUNKS):
                for piece, held in ((0, high), (1, low)):
                    rows = pl.ds((2 * piece + part) * chunk, chunk)
                    table[w, rows, a * LANES : (a + 1) * LANES] = held[w * chunk : (w + 1) * chunk]


def transform_chunk(w, hist, table, sums, buf, me):
    blocks, exc, length = hist.shape[0], hist.shape[1], hist.shape[2]
    half = table.shape[1] // 2
    chunk = half // 2
    for e in range(0, exc, 2):
        value = None
        for f in range(blocks):
            steps = jnp.concatenate([hist[f, e], hist[f, e + 1]], axis=1)
            term = dot(table[w, :, f * length : (f + 1) * length], steps, NN)
            value = term if value is None else value + term
        value = value[:half] + value[half:]
        for part in range(2):
            for side in range(2):
                sums[pl.ds(part * exc + e + side, chunk, stride=2 * exc), :] = value[
                    part * chunk : (part + 1) * chunk, side * LANES : (side + 1) * LANES
                ]
    buf[me, pl.ds(0, chunk)] = sums[...].reshape(chunk, 2 * exc, LANES).astype(jnp.bfloat16)


def compress_chunk(w, buf, coeffs, basis_in, me, chunk):
    rows, rank = buf.shape[2], basis_in.shape[2]
    half = rows // 2
    pack = LANES // rank
    lane = lax.broadcasted_iota(jnp.int32, (rows, LANES), 1) // rank

    def step(group, carry):
        left = buf[me, pl.ds(group * pack, pack)].reshape(pack * rows, LANES)

        def pick(part):
            right = basis_in[pl.ds(w * chunk + group * pack, pack), part]
            full = dot(left, right.reshape(pack * rank, LANES), NT)
            out = full[:rows]
            for i in range(1, pack):
                out = jnp.where(lane == i, full[i * rows : (i + 1) * rows], out)
            return out

        by_re, by_im = pick(0), pick(1)
        real = by_re[:half] - by_im[half:]
        imag = by_re[half:] + by_im[:half]
        coeffs[me, w * (chunk // pack) + group] = jnp.concatenate([real, imag], 0).astype(jnp.bfloat16)
        return carry

    lax.fori_loop(0, chunk // pack, step, 0)


def far_groups(first, count, coeffs, couple, basis_out, limit, far):
    rank = couple.shape[2]
    sources, rows = coeffs.shape[0], coeffs.shape[2]
    half = rows // 2
    pack = LANES // rank
    unroll = min(2, count)
    position = lax.broadcasted_iota(jnp.int32, (rank, sources * rank), 0)

    def step(pair, carry):
        groups = [first + pair * unroll + u for u in range(unroll)]
        waves = [(g * pack + i, i, u) for u, g in enumerate(groups) for i in range(pack)]
        packed = [[coeffs[s, g].astype(jnp.float32) for s in range(sources)] for g in groups]
        stacked = [
            jnp.concatenate([p[:, i * rank : (i + 1) * rank] for p in packed[u]], axis=1).astype(jnp.bfloat16)
            for _, i, u in waves
        ]
        mixes = []
        for (wave, _, _), left in zip(waves, stacked):
            keep = position < limit[pl.ds(wave, 1), :]
            parts = [couple[wave, part] for part in range(2)]
            mixes.append([dot(left, jnp.where(keep, v, jnp.zeros_like(v)), NT) for v in parts])
        mixed = [
            jnp.concatenate([r[:half] - m[half:], r[half:] + m[:half]], 0).astype(jnp.bfloat16)
            for r, m in mixes
        ]
        spread = [[dot(m, basis_out[wave, part], NN) for part in range(2)] for (wave, _, _), m in zip(waves, mixed)]
        for (wave, _, _), (r, m) in zip(waves, spread):
            far[wave, pl.ds(0, half)] = r[:half] - m[half:]
            far[wave, pl.ds(half, half)] = r[half:] + m[:half]
        return carry

    lax.fori_loop(0, count // unroll, step, 0)


def near_chunk(w, picked, near, buf, far, out):
    slots, chunk = near.shape[1], near.shape[2]
    panels = near.shape[4]
    half = buf.shape[2] // 2
    unroll = 4

    def step(group, carry):
        waves = [group * unroll + i for i in range(unroll)]
        sums = []
        for k in waves:
            left = jnp.concatenate([buf[s, k] for s in picked], axis=1)
            right = jnp.concatenate(
                [near[w, j, k].reshape(2 * panels, panels) for j in range(slots)], axis=1
            )
            sums.append(dot(left, right, NT))
        for k, both in zip(waves, sums):
            by_re, by_im = both[:, :panels], both[:, panels:]
            wave = w * chunk + k
            out[wave, 0] = (by_re[:half] - by_im[half:] + far[wave, pl.ds(0, half)]).astype(out.dtype)
            out[wave, 1] = (by_re[half:] + by_im[:half] + far[wave, pl.ds(half, half)]).astype(out.dtype)
        return carry

    lax.fori_loop(0, chunk // unroll, step, 0)


def kernel(freqs, clusters, mine, c_re, c_im, f_re, f_im, limit, own, near_in, couple_in, out_in, in_in,
           out, hist, table, sums, near, couple, basis_out, basis_in, *rest):
    bufs = rest[: CHUNKS + 1]
    coeffs = bufs[CHUNKS]
    far, local_sem, near_sem, hist_send, hist_recv, send_sem, recv_sem = rest[CHUNKS + 1 :]
    f, c = lax.axis_index("freq"), lax.axis_index("clus")
    z, core = c // 2, c % 2
    levels = clusters // 2
    has_up, has_down = z + 1 < levels, z > 0
    up, down, partner = c + 2, c - 2, c + 1 - 2 * core
    chunk = near.shape[2]
    square = freqs == 4
    beside, across = f + 1 - 2 * (f % 2), (f + 2) % freqs
    peers = [beside, across] if square else [(f + i) % freqs for i in range(1, freqs)]

    loads = [
        pltpu.make_async_copy(own, hist.at[f], local_sem.at[0]),
        pltpu.make_async_copy(in_in, basis_in, local_sem.at[1]),
        pltpu.make_async_copy(out_in, basis_out, local_sem.at[2]),
        pltpu.make_async_copy(couple_in.at[0], couple, local_sem.at[3]),
    ]
    blocks = [
        pltpu.make_async_copy(near_in.at[0, :, pl.ds(w * chunk, chunk)], near.at[w], near_sem.at[w])
        for w in range(CHUNKS)
    ]

    barrier = pltpu.get_barrier_semaphore()
    for peer in peers:
        pl.semaphore_signal(barrier, inc=1, device_id=(peer, c), device_id_type=MESH)
    pl.semaphore_signal(barrier, inc=1, device_id=(f, partner), device_id_type=MESH)

    @pl.when(has_up)
    def _():
        pl.semaphore_signal(barrier, inc=1, device_id=(f, up), device_id_type=MESH)

    @pl.when(has_down)
    def _():
        pl.semaphore_signal(barrier, inc=1, device_id=(f, down), device_id_type=MESH)

    loads[0].start()
    pl.semaphore_wait(barrier, len(peers) + 1 + jnp.where(z + 1 < levels, 1, 0) + jnp.where(z > 0, 1, 0))

    exc = own.shape[0]
    halves = [pl.ds(0, exc // 2), pl.ds(exc // 2, exc // 2)]

    def give(peer, slot, part, source, number):
        return pltpu.make_async_remote_copy(
            src_ref=source, dst_ref=hist.at[slot, halves[part]],
            send_sem=hist_send.at[number], recv_sem=hist_recv.at[slot, part],
            device_id=(peer, c), device_id_type=MESH,
        )

    def arrived(slot, part):
        give(peers[0], slot, part, hist.at[slot, halves[part]], 0).wait_recv()

    sent = []
    for number, peer in enumerate(peers):
        for part in ((0, 1) if number % 2 == 0 else (1, 0)):
            sent.append(give(peer, f, part, own.at[halves[part]], 2 * number + part))
            sent[-1].start()
    for copy in loads[1:] + blocks:
        copy.start()
    fill_tables(c_re, c_im, f_re, f_im, table)
    if square:
        arrived(beside, 0)
        sent.append(give(across, beside, 0, hist.at[beside, halves[0]], 4))
        sent[-1].start()
        arrived(across, 1)
        sent.append(give(beside, across, 1, hist.at[across, halves[1]], 5))
        sent[-1].start()
        corner = (beside + 2) % freqs
        for slot, part in ((beside, 1), (across, 0), (corner, 0), (corner, 1)):
            arrived(slot, part)
    else:
        for peer in peers:
            for part in range(2):
                arrived(peer, part)
    for copy in sent:
        copy.wait_send()
    loads[0].wait()
    loads[1].wait()

    def pass_on(w, source, target, way):
        return pltpu.make_async_remote_copy(
            src_ref=bufs[w].at[source], dst_ref=bufs[w].at[source],
            send_sem=send_sem.at[w, source // 2, way], recv_sem=recv_sem.at[w, source],
            device_id=(f, target), device_id_type=MESH,
        )

    def when(flag, action):
        @pl.when(flag)
        def _():
            action()

    def send_own(w):
        when(has_up, lambda: pass_on(w, c, up, 0).start())
        when(has_down, lambda: pass_on(w, c, down, 1).start())
        pass_on(w, c, partner, 2).start()

    early = CHUNKS // 2
    for w in range(CHUNKS):
        transform_chunk(w, hist, table, sums, bufs[w], c)
        if w < early:
            send_own(w)
    for w in range(CHUNKS):
        compress_chunk(w, bufs[w], coeffs, basis_in, c, chunk)
    for w in [CHUNKS] + list(range(early, CHUNKS)):
        send_own(w)

    for copy in loads[2:]:
        copy.wait()
    picked = [mine[j] for j in range(near.shape[1])]
    order = [CHUNKS] + list(range(CHUNKS))

    def relay(w, d):
        below, above = c - 2 * d, c + 2 * d

        def from_below():
            pass_on(w, below, partner, 2).wait_recv()
            when(has_up, lambda: pass_on(w, below, up, 0).start())
            pass_on(w, below, partner, 2).start()

        def from_above():
            pass_on(w, above, partner, 2).wait_recv()
            when(has_down, lambda: pass_on(w, above, down, 1).start())
            pass_on(w, above, partner, 2).start()

        when(z >= d, from_below)
        when(z + d < levels, from_above)

    def complete(w):
        pass_on(w, partner, partner, 2).wait_recv()
        for d in range(1, levels):
            below, above = partner - 2 * d, partner + 2 * d
            when(z >= d, lambda: pass_on(w, below, partner, 2).wait_recv())
            when(z + d < levels, lambda: pass_on(w, above, partner, 2).wait_recv())

    for d in range(1, levels - 1):
        for w in order:
            relay(w, d)
    relay(CHUNKS, levels - 1)
    complete(CHUNKS)
    groups = coeffs.shape[1] // CHUNKS
    for w in range(CHUNKS):
        far_groups(w * groups, groups, coeffs, couple, basis_out, limit, far)
        relay(w, levels - 1)
    for w in range(CHUNKS):
        complete(w)
        blocks[w].wait()
        near_chunk(w, picked, near, bufs[w], far, out)

    for w in order:
        when(has_up, lambda: pass_on(w, c, up, 0).wait_send())
        when(has_down, lambda: pass_on(w, c, down, 1).wait_send())
        pass_on(w, c, partner, 2).wait_send()
        for d in range(1, levels):
            below, above = c - 2 * d, c + 2 * d

            def below_sent():
                when(has_up, lambda: pass_on(w, below, up, 0).wait_send())
                pass_on(w, below, partner, 2).wait_send()

            def above_sent():
                when(has_down, lambda: pass_on(w, above, down, 1).wait_send())
                pass_on(w, above, partner, 2).wait_send()

            when(z >= d, below_sent)
            when(z + d < levels, above_sent)


def step_all(mine, factors, limit, turned, near_blocks, coupling, basis_out, basis_in, freqs, clusters):
    exc, length, panels = turned.shape
    waves, _, rank, _ = basis_in.shape
    slots = near_blocks.shape[1]
    chunk = waves // CHUNKS
    pack = LANES // rank
    rows = 2 * exc
    bf16 = jnp.bfloat16
    vmem, anywhere = pl.BlockSpec(memory_space=pltpu.VMEM), pl.BlockSpec(memory_space=pl.ANY)
    dma = pltpu.SemaphoreType.DMA
    return pl.pallas_call(
        functools.partial(kernel, freqs, clusters),
        out_shape=jax.ShapeDtypeStruct((waves, 2, exc, panels), bf16),
        in_specs=[pl.BlockSpec(memory_space=pltpu.SMEM)] + [vmem] * 6 + [anywhere] * 4,
        out_specs=vmem,
        scratch_shapes=[
            pltpu.VMEM((freqs, exc, length, panels), bf16),
            pltpu.VMEM((CHUNKS, 4 * chunk, freqs * length), bf16),
            pltpu.VMEM((chunk * rows, panels), jnp.float32),
            pltpu.VMEM((CHUNKS, slots, chunk, 2, panels, panels), bf16),
            pltpu.VMEM(coupling.shape[1:], bf16),
            pltpu.VMEM(basis_out.shape, bf16),
            pltpu.VMEM(basis_in.shape, bf16),
        ]
        + [pltpu.VMEM((clusters, chunk, rows, panels), bf16)] * CHUNKS
        + [
            pltpu.VMEM((clusters, waves // pack, rows, LANES), bf16),
            pltpu.VMEM((waves, rows, panels), jnp.float32),
            dma((4,)),
            dma((CHUNKS,)),
            dma((max(6, 2 * freqs),)),
            dma((freqs, 2)),
            dma((CHUNKS + 1, clusters // 2, 3)),
            dma((CHUNKS + 1, clusters)),
        ],
        compiler_params=pltpu.CompilerParams(
            collective_id=0, has_side_effects=True, vmem_limit_bytes=60 * 1024 * 1024
        ),
    )(mine, *factors, limit, turned, near_blocks, coupling, basis_out, basis_in)


def local(history, near_blocks, near_list, basis_out, basis_in, coupling, ranks):
    steps_dev, exc, panels = history.shape
    waves_dev, _, rank, _ = basis_in.shape
    clusters = lax.axis_size("clus")
    freqs = lax.axis_size("freq")
    total = steps_dev * freqs
    mine = lax.dynamic_index_in_dim(near_list, lax.axis_index("clus"), 0, keepdims=False)
    nearby = jnp.any(mine[:, None] == lax.iota(jnp.int32, clusters)[None, :], axis=0)
    far = jnp.where(nearby[None, :], 0, ranks[0])
    within = lax.iota(jnp.int32, rank)
    limit = jnp.where(within[None, None, :] < far[:, :, None], far[:, :, None], 0)
    limit = limit.reshape(waves_dev, clusters * rank)
    factors = wave_factors(lax.axis_index("freq") * waves_dev, waves_dev, total)
    turned = jnp.transpose(history, (1, 0, 2))
    return step_all(
        mine, factors, limit, turned, near_blocks, coupling, basis_out, basis_in, freqs, clusters
    )


def solution(mesh):
    placed = (
        P("freq", None, "clus"),
        P("clus", None, "freq", None, None, None),
        P(),
        P("freq", None, None, "clus"),
        P("freq", None, None, "clus"),
        P("clus", "freq", None, None, None),
        P("clus", "freq", None),
    )
    return jax.shard_map(
        local, mesh=mesh, in_specs=placed, out_specs=P("freq", None, None, "clus"), check_vma=False
    )
```

```python
import functools
import math

import jax
import jax.numpy as jnp
from jax import lax
from jax.experimental import pallas as pl
from jax.experimental.pallas import tpu as pltpu
from jax.sharding import PartitionSpec as P

LANES = 128
NT = (((1,), (1,)), ((), ()))
NN = (((1,), (0,)), ((), ()))


def dot(left, right, dims):
    return lax.dot_general(left, right, dims, preferred_element_type=jnp.float32)


def wave_factors(first_wave, count, total):
    waves = (first_wave + lax.iota(jnp.int32, count))[:, None]

    def factor(steps, scale):
        angle = (waves * steps[None, :] % total).astype(jnp.float32) * (2.0 * math.pi / total)
        weight = jnp.exp(steps.astype(jnp.float32) * (-math.log(2.0) / total)) * scale
        return weight[None, :] * jnp.cos(angle), -weight[None, :] * jnp.sin(angle)

    coarse = factor(lax.iota(jnp.int32, total // LANES) * LANES, 1.0)
    fine = factor(lax.iota(jnp.int32, LANES), total ** (-0.5))
    return coarse + fine


CHUNKS = 4
MESH = pl.DeviceIdType.MESH


def fill_tables(coarse_re, coarse_im, fine_re, fine_im, table):
    waves = fine_re.shape[0]
    chunk = waves // CHUNKS
    for a in range(coarse_re.shape[1]):
        c_re, c_im = coarse_re[:, a : a + 1], coarse_im[:, a : a + 1]
        f_re, f_im = fine_re[...], fine_im[...]
        for part, value in ((0, c_re * f_re - c_im * f_im), (1, c_re * f_im + c_im * f_re)):
            high = value.astype(jnp.bfloat16)
            low = (value - high.astype(jnp.float32)).astype(jnp.bfloat16)
            for w in range(CHUNKS):
                for piece, held in ((0, high), (1, low)):
                    rows = pl.ds((2 * piece + part) * chunk, chunk)
                    table[w, rows, a * LANES : (a + 1) * LANES] = held[w * chunk : (w + 1) * chunk]


def join(by_re, by_im, quarter):
    real = [r[:quarter] - m[quarter:] for r, m in zip(by_re, by_im)]
    imag = [r[quarter:] + m[:quarter] for r, m in zip(by_re, by_im)]
    return jnp.concatenate(real, 0), jnp.concatenate(imag, 0)


def transform_chunk(w, h, hist, table, sums, buf, me):
    blocks, exc, length = hist.shape[0], hist.shape[1], hist.shape[2]
    half = table.shape[1] // 2
    chunk = half // 2
    quarter = exc // 2
    for e in range(0, quarter, 2):
        value = None
        for f in range(blocks):
            steps = jnp.concatenate([hist[f, h * quarter + e], hist[f, h * quarter + e + 1]], axis=1)
            term = dot(table[w, :, f * length : (f + 1) * length], steps, NN)
            value = term if value is None else value + term
        value = value[:half] + value[half:]
        for part in range(2):
            for side in range(2):
                sums[pl.ds(part * quarter + e + side, chunk, stride=exc), :] = value[
                    part * chunk : (part + 1) * chunk, side * LANES : (side + 1) * LANES
                ]
    buf[me] = sums[...].reshape(chunk, exc, LANES).astype(jnp.bfloat16)


def compress_chunk(w, pair, coeffs, basis_in, me):
    chunk, exc, rank = pair[0].shape[1], pair[0].shape[2], basis_in.shape[2]
    pack = LANES // rank
    lane = lax.broadcasted_iota(jnp.int32, (exc, LANES), 1) // rank

    def step(group, carry):
        left = jnp.concatenate(
            [buf[me, pl.ds(group * pack, pack)].reshape(pack * exc, LANES) for buf in pair], axis=0
        )

        def pick(part):
            right = basis_in[pl.ds(w * chunk + group * pack, pack), part]
            full = dot(left, right.reshape(pack * rank, LANES), NT)
            outs = []
            for h in range(2):
                rows = full[h * pack * exc : (h + 1) * pack * exc]
                out = rows[:exc]
                for i in range(1, pack):
                    out = jnp.where(lane == i, rows[i * exc : (i + 1) * exc], out)
                outs.append(out)
            return outs

        real, imag = join(pick(0), pick(1), exc // 2)
        coeffs[me, w * (chunk // pack) + group] = jnp.concatenate([real, imag], 0).astype(jnp.bfloat16)
        return carry

    lax.fori_loop(0, chunk // pack, step, 0)


def far_groups(first, count, coeffs, couple, basis_out, limit, far):
    rank = couple.shape[2]
    sources, rows = coeffs.shape[0], coeffs.shape[2]
    half = rows // 2
    pack = LANES // rank
    unroll = min(2, count)
    position = lax.broadcasted_iota(jnp.int32, (rank, sources * rank), 0)

    def step(pair, carry):
        groups = [first + pair * unroll + u for u in range(unroll)]
        waves = [(g * pack + i, i, u) for u, g in enumerate(groups) for i in range(pack)]
        packed = [[coeffs[s, g].astype(jnp.float32) for s in range(sources)] for g in groups]
        stacked = [
            jnp.concatenate([p[:, i * rank : (i + 1) * rank] for p in packed[u]], axis=1).astype(jnp.bfloat16)
            for _, i, u in waves
        ]
        mixes = []
        for (wave, _, _), left in zip(waves, stacked):
            keep = position < limit[pl.ds(wave, 1), :]
            parts = [couple[wave, part] for part in range(2)]
            mixes.append([dot(left, jnp.where(keep, v, jnp.zeros_like(v)), NT) for v in parts])
        mixed = [
            jnp.concatenate([r[:half] - m[half:], r[half:] + m[:half]], 0).astype(jnp.bfloat16)
            for r, m in mixes
        ]
        spread = [[dot(m, basis_out[wave, part], NN) for part in range(2)] for (wave, _, _), m in zip(waves, mixed)]
        for (wave, _, _), (r, m) in zip(waves, spread):
            far[wave, pl.ds(0, half)] = r[:half] - m[half:]
            far[wave, pl.ds(half, half)] = r[half:] + m[:half]
        return carry

    lax.fori_loop(0, count // unroll, step, 0)


def near_chunk(w, picked, near, pair, far, out):
    slots, chunk = near.shape[1], near.shape[2]
    panels = near.shape[4]
    exc = pair[0].shape[2]
    unroll = 4

    def step(group, carry):
        waves = [group * unroll + i for i in range(unroll)]
        sums = []
        for k in waves:
            left = jnp.concatenate(
                [jnp.concatenate([buf[s, k] for s in picked], axis=1) for buf in pair], axis=0
            )
            right = jnp.concatenate(
                [near[w, j, k].reshape(2 * panels, panels) for j in range(slots)], axis=1
            )
            sums.append(dot(left, right, NT))
        for k, both in zip(waves, sums):
            by_re = [both[:exc, :panels], both[exc:, :panels]]
            by_im = [both[:exc, panels:], both[exc:, panels:]]
            real, imag = join(by_re, by_im, exc // 2)
            wave = w * chunk + k
            out[wave, 0] = (real + far[wave, pl.ds(0, exc)]).astype(out.dtype)
            out[wave, 1] = (imag + far[wave, pl.ds(exc, exc)]).astype(out.dtype)
        return carry

    lax.fori_loop(0, chunk // unroll, step, 0)


def kernel(freqs, clusters, mine, c_re, c_im, f_re, f_im, limit, own, near_in, couple_in, out_in, in_in,
           out, hist, table, sums, near, couple, basis_out, basis_in, *rest):
    total = 2 * CHUNKS
    bufs = rest[: total + 1]
    coeffs = bufs[total]
    far, local_sem, near_sem, hist_send, hist_recv, send_sem, recv_sem = rest[total + 1 :]
    f, c = lax.axis_index("freq"), lax.axis_index("clus")
    z, core = c // 2, c % 2
    levels = clusters // 2
    has_up, has_down = z + 1 < levels, z > 0
    up, down, partner = c + 2, c - 2, c + 1 - 2 * core
    chunk = near.shape[2]
    square = freqs == 4
    beside, across = f + 1 - 2 * (f % 2), (f + 2) % freqs
    peers = [beside, across] if square else [(f + i) % freqs for i in range(1, freqs)]

    loads = [
        pltpu.make_async_copy(own, hist.at[f], local_sem.at[0]),
        pltpu.make_async_copy(in_in, basis_in, local_sem.at[1]),
        pltpu.make_async_copy(out_in, basis_out, local_sem.at[2]),
        pltpu.make_async_copy(couple_in.at[0], couple, local_sem.at[3]),
    ]
    blocks = [
        pltpu.make_async_copy(near_in.at[0, :, pl.ds(w * chunk, chunk)], near.at[w], near_sem.at[w])
        for w in range(CHUNKS)
    ]

    barrier = pltpu.get_barrier_semaphore()
    for peer in peers:
        pl.semaphore_signal(barrier, inc=1, device_id=(peer, c), device_id_type=MESH)
    pl.semaphore_signal(barrier, inc=1, device_id=(f, partner), device_id_type=MESH)

    @pl.when(has_up)
    def _():
        pl.semaphore_signal(barrier, inc=1, device_id=(f, up), device_id_type=MESH)

    @pl.when(has_down)
    def _():
        pl.semaphore_signal(barrier, inc=1, device_id=(f, down), device_id_type=MESH)

    loads[0].start()
    pl.semaphore_wait(barrier, len(peers) + 1 + jnp.where(z + 1 < levels, 1, 0) + jnp.where(z > 0, 1, 0))

    quarter = own.shape[0] // 4
    pieces = [pl.ds(q * quarter, quarter) for q in range(4)]

    def give(peer, slot, part, source, number):
        return pltpu.make_async_remote_copy(
            src_ref=source.at[pieces[part]], dst_ref=hist.at[slot, pieces[part]],
            send_sem=hist_send.at[number, part], recv_sem=hist_recv.at[slot, part],
            device_id=(peer, c), device_id_type=MESH,
        )

    def arrived(slot, part):
        give(peers[0], slot, part, hist.at[slot], 0).wait_recv()

    sent = []

    def send(*what):
        sent.append(give(*what))
        sent[-1].start()

    def give_half(h):
        for i in range(2):
            for number, peer in enumerate(peers):
                part = 2 * h + (i + number) % 2
                send(peer, f, part, own, number)

    def relay_half(h):
        if square:
            arrived(beside, 2 * h)
            send(across, beside, 2 * h, hist.at[beside], len(peers))
            arrived(across, 2 * h + 1)
            send(beside, across, 2 * h + 1, hist.at[across], len(peers))

    def finish_half(h):
        if square:
            corner = (beside + 2) % freqs
            order = [(beside, 1), (across, 0), (corner, 0), (corner, 1)]
        else:
            order = [(peer, part) for peer in peers for part in range(2)]
        for slot, part in order:
            arrived(slot, 2 * h + part)

    give_half(0)
    for copy in loads[1:] + blocks:
        copy.start()
    fill_tables(c_re, c_im, f_re, f_im, table)
    relay_half(0)
    give_half(1)
    finish_half(0)
    loads[0].wait()

    def pass_on(w, source, target, way):
        return pltpu.make_async_remote_copy(
            src_ref=bufs[w].at[source], dst_ref=bufs[w].at[source],
            send_sem=send_sem.at[w, source // 2, way], recv_sem=recv_sem.at[w, source],
            device_id=(f, target), device_id_type=MESH,
        )

    def when(flag, action):
        @pl.when(flag)
        def _():
            action()

    def send_own(w):
        when(has_up, lambda: pass_on(w, c, up, 0).start())
        when(has_down, lambda: pass_on(w, c, down, 1).start())
        pass_on(w, c, partner, 2).start()

    def relay(w, d):
        below, above = c - 2 * d, c + 2 * d

        def from_below():
            pass_on(w, below, partner, 2).wait_recv()
            when(has_up, lambda: pass_on(w, below, up, 0).start())
            pass_on(w, below, partner, 2).start()

        def from_above():
            pass_on(w, above, partner, 2).wait_recv()
            when(has_down, lambda: pass_on(w, above, down, 1).start())
            pass_on(w, above, partner, 2).start()

        when(z >= d, from_below)
        when(z + d < levels, from_above)

    def complete(w):
        pass_on(w, partner, partner, 2).wait_recv()
        for d in range(1, levels):
            below, above = partner - 2 * d, partner + 2 * d
            when(z >= d, lambda: pass_on(w, below, partner, 2).wait_recv())
            when(z + d < levels, lambda: pass_on(w, above, partner, 2).wait_recv())

    first, second = [2 * w for w in range(CHUNKS)], [2 * w + 1 for w in range(CHUNKS)]
    for w in range(CHUNKS):
        transform_chunk(w, 0, hist, table, sums, bufs[first[w]], c)
        send_own(first[w])
    relay_half(1)
    if levels > 1:
        for m in first:
            relay(m, 1)
    finish_half(1)
    for w in range(CHUNKS):
        transform_chunk(w, 1, hist, table, sums, bufs[second[w]], c)
        send_own(second[w])
    loads[1].wait()
    for w in range(CHUNKS):
        compress_chunk(w, (bufs[first[w]], bufs[second[w]]), coeffs, basis_in, c)
    send_own(total)
    for copy in loads[2:]:
        copy.wait()
    picked = [mine[j] for j in range(near.shape[1])]
    last = levels - 1
    for d in range(1, last):
        if d > 1:
            for m in first:
                relay(m, d)
            for m in [total] + second:
                relay(m, d)
        else:
            for m in second[:2] + [total] + second[2:]:
                relay(m, d)
    if last > 1:
        for m in first:
            relay(m, last)
    relay(total, last)
    complete(total)
    groups = coeffs.shape[1] // CHUNKS
    for w in range(CHUNKS):
        far_groups(w * groups, groups, coeffs, couple, basis_out, limit, far)
        relay(second[w], last)
    for w in range(CHUNKS):
        complete(first[w])
        complete(second[w])
        blocks[w].wait()
        near_chunk(w, picked, near, (bufs[first[w]], bufs[second[w]]), far, out)

    for copy in sent:
        copy.wait_send()
    for w in range(total + 1):
        when(has_up, lambda: pass_on(w, c, up, 0).wait_send())
        when(has_down, lambda: pass_on(w, c, down, 1).wait_send())
        pass_on(w, c, partner, 2).wait_send()
        for d in range(1, levels):
            below, above = c - 2 * d, c + 2 * d

            def below_sent():
                when(has_up, lambda: pass_on(w, below, up, 0).wait_send())
                pass_on(w, below, partner, 2).wait_send()

            def above_sent():
                when(has_down, lambda: pass_on(w, above, down, 1).wait_send())
                pass_on(w, above, partner, 2).wait_send()

            when(z >= d, below_sent)
            when(z + d < levels, above_sent)


def step_all(mine, factors, limit, turned, near_blocks, coupling, basis_out, basis_in, freqs, clusters):
    exc, length, panels = turned.shape
    waves, _, rank, _ = basis_in.shape
    slots = near_blocks.shape[1]
    chunk = waves // CHUNKS
    pack = LANES // rank
    rows = 2 * exc
    bf16 = jnp.bfloat16
    vmem, anywhere = pl.BlockSpec(memory_space=pltpu.VMEM), pl.BlockSpec(memory_space=pl.ANY)
    dma = pltpu.SemaphoreType.DMA
    return pl.pallas_call(
        functools.partial(kernel, freqs, clusters),
        out_shape=jax.ShapeDtypeStruct((waves, 2, exc, panels), bf16),
        in_specs=[pl.BlockSpec(memory_space=pltpu.SMEM)] + [vmem] * 6 + [anywhere] * 4,
        out_specs=vmem,
        scratch_shapes=[
            pltpu.VMEM((freqs, exc, length, panels), bf16),
            pltpu.VMEM((CHUNKS, 4 * chunk, freqs * length), bf16),
            pltpu.VMEM((chunk * exc, panels), jnp.float32),
            pltpu.VMEM((CHUNKS, slots, chunk, 2, panels, panels), bf16),
            pltpu.VMEM(coupling.shape[1:], bf16),
            pltpu.VMEM(basis_out.shape, bf16),
            pltpu.VMEM(basis_in.shape, bf16),
        ]
        + [pltpu.VMEM((clusters, chunk, exc, panels), bf16)] * (2 * CHUNKS)
        + [
            pltpu.VMEM((clusters, waves // pack, rows, LANES), bf16),
            pltpu.VMEM((waves, rows, panels), jnp.float32),
            dma((4,)),
            dma((CHUNKS,)),
            dma((freqs, 4)),
            dma((freqs, 4)),
            dma((2 * CHUNKS + 1, clusters // 2, 3)),
            dma((2 * CHUNKS + 1, clusters)),
        ],
        compiler_params=pltpu.CompilerParams(
            collective_id=0, has_side_effects=True, vmem_limit_bytes=60 * 1024 * 1024
        ),
    )(mine, *factors, limit, turned, near_blocks, coupling, basis_out, basis_in)


def local(history, near_blocks, near_list, basis_out, basis_in, coupling, ranks):
    steps_dev, exc, panels = history.shape
    waves_dev, _, rank, _ = basis_in.shape
    clusters = lax.axis_size("clus")
    freqs = lax.axis_size("freq")
    total = steps_dev * freqs
    mine = lax.dynamic_index_in_dim(near_list, lax.axis_index("clus"), 0, keepdims=False)
    nearby = jnp.any(mine[:, None] == lax.iota(jnp.int32, clusters)[None, :], axis=0)
    far = jnp.where(nearby[None, :], 0, ranks[0])
    within = lax.iota(jnp.int32, rank)
    limit = jnp.where(within[None, None, :] < far[:, :, None], far[:, :, None], 0)
    limit = limit.reshape(waves_dev, clusters * rank)
    factors = wave_factors(lax.axis_index("freq") * waves_dev, waves_dev, total)
    turned = jnp.transpose(history, (1, 0, 2))
    return step_all(
        mine, factors, limit, turned, near_blocks, coupling, basis_out, basis_in, freqs, clusters
    )


def solution(mesh):
    placed = (
        P("freq", None, "clus"),
        P("clus", None, "freq", None, None, None),
        P(),
        P("freq", None, None, "clus"),
        P("freq", None, None, "clus"),
        P("clus", "freq", None, None, None),
        P("clus", "freq", None),
    )
    return jax.shard_map(
        local, mesh=mesh, in_specs=placed, out_specs=P("freq", None, None, "clus"), check_vma=False
    )
```
